256 devices in a mesh: tok: 32 (over z, y), voc: 8 (over x, core).
Axes of the slice: x: 4, y: 4, z: 8, core: 2. Of those that a mesh axis runs over, the one named last changes fastest.
Arguments:
- hidden: bfloat16 [8192, 1536], P('tok'), may hold values from -1000 to 1000
- norm_gain: float32 [1536], replicated, may hold values from 0.1 to 1.9
- head_weight: bfloat16 [1536, 49152], P(None, ('tok', 'voc')), may hold values from -8 to 8
- targets: int32 [8192], P('tok'), may hold values from 0 to 49151
- lengths: int32 [32], replicated, may hold values from 1 to 256, 5120 in all
- prior_device: int32 [32], replicated, may hold values from 0 to 31, each once
- prior_row: int32 [32], replicated, may hold values from 0 to 255
Outputs:
- logprob: float32 [8192], P('tok')
- entropy: float32 [8192], P('tok')
The draws below stay inside these ranges and needn't reach their ends.
Inputs may be any that keep to these rules, and one draw needn't show every extreme that they name: One turn's block is full, lengths[t] = 256. `prior_device`: every block index appears once.
All inputs are finite; a program needn't handle non-finite values.
Results may differ from the reference program's by a relative error of at most 0.0036.
Values may be sent and summed in bfloat16 or wider, within the bound.
A program may use at most 192 MiB of HBM per device.

```python
import math
import jax
import jax.numpy as jnp
import numpy as np
from jax import lax

D = 1536
V = 49152
TOK_DEV = 256
TURNS = 32
TOKENS = 8192
LIVE_TOTAL = 5120


def drawn_dirs(key):
    return jnp.sign(jax.random.normal(jax.random.fold_in(key, 77), (8, 4, D), jnp.float32) + 0.001)


def draw_head_weight(key, part):
    noise = jnp.clip(jax.random.normal(jax.random.fold_in(key, 1), (D, V), jnp.float32), -5.0, 5.0)
    feature_scale = jnp.exp(jax.random.uniform(jax.random.fold_in(key, 8), (D, 1), jnp.float32) * math.log(4.0)) / 2.326
    spread = jnp.exp(jax.random.uniform(jax.random.fold_in(key, 2), (1, V), jnp.float32) * math.log(1.2))
    ramp = 0.9 + 0.2 * jnp.arange(V, dtype=jnp.float32)[None, :] / V
    weight = noise * feature_scale * spread * ramp * (3.8 / math.sqrt(D))
    direct = drawn_dirs(key).reshape(32, D).T
    strength = np.tile(1.0 + 0.5 * np.arange(4), 8)
    columns = np.array([j * (V // 8) + 2 * m for j in range(8) for m in range(4)])
    leading = direct * jnp.asarray(123.0 * strength / D, jnp.float32)[None, :]
    partner = leading * jnp.asarray(1.0 - 2.0 / (123.0 * strength), jnp.float32)[None, :]
    weight = weight.at[:, columns].set(leading).at[:, columns + 1].set(partner)
    return weight.astype(jnp.bfloat16)


def draw_hidden(key, part):
    noise = jnp.clip(jax.random.normal(jax.random.fold_in(key, 3), (TOKENS, D), jnp.float32), -5.0, 5.0)
    row_scale = jnp.exp(jax.random.uniform(jax.random.fold_in(key, 4), (TOKENS, 1), jnp.float32) * math.log(10.0))
    col_scale = jnp.exp(jax.random.uniform(jax.random.fold_in(key, 5), (1, D), jnp.float32) * math.log(10.0))
    values = noise * row_scale * col_scale
    turn_count = TOKENS // TOK_DEV
    rows = np.array([t * TOK_DEV + m for t in range(turn_count) for m in range(4)])
    first_ids = np.array([t % 8 for t in range(turn_count) for m in range(4)])
    second_ids = np.array([m for t in range(turn_count) for m in range(4)])
    direct = drawn_dirs(key)[first_ids, second_ids]
    values = values.at[rows].set(direct)
    return values.astype(jnp.bfloat16)


def plant(values, key, low, high):
    spot = [jax.random.randint(jax.random.fold_in(key, axis), (), 0, length) for axis, length in enumerate(values.shape)]
    main_axis = values.shape.index(max(values.shape))
    neighbour = spot[:main_axis] + [(spot[main_axis] + 1) % values.shape[main_axis]] + spot[main_axis + 1:]
    return values.at[tuple(spot)].set(low).at[tuple(neighbour)].set(high)


def rank_bounds(count, slope):
    loads = [(1 << 20) // math.isqrt(grade ** slope) + 1 for grade in range(1, count + 1)]
    scale = 1 + sum(loads) // (1 << 30)
    return np.cumsum(np.array([max(1, weight // scale) for weight in loads]))


def ranked(key, extent, number_of, lean):
    grid = rank_bounds(number_of, lean)
    lot = jax.random.randint(jax.random.fold_in(key, 1), extent, 0, int(grid[number_of - 1]))
    standing = jnp.searchsorted(jnp.asarray(grid, jnp.int32), lot, side="right")
    return jax.random.permutation(jax.random.fold_in(key, 2), number_of)[standing].astype(jnp.int32)


def length_profile(amount, total, limit, skew):
    weights = [(1 << 20) // math.isqrt(grade ** skew) + 1 for grade in range(2, amount + 1)]
    rest, given = total - limit - (amount - 1), [1] * (amount - 1)
    while rest > 0:
        candidates = [i for i in range(amount - 1) if given[i] < limit]
        whole, remaining = sum([weights[i] for i in candidates]), rest
        for i in candidates:
            addition = min(limit - given[i], max(1, remaining * weights[i] // whole), rest)
            given[i] = given[i] + addition
            rest = rest - addition
    return np.array([limit] + given)


def ragged(stream_key, number_of, total, most, lean):
    if number_of == 2:
        one = jax.random.randint(stream_key, (), max(1, total - most), min(most, total - 1) + 1)
        return jnp.stack([one, total - one])
    sizes = jnp.asarray(length_profile(number_of, total, most, lean), jnp.int32)
    twos = (number_of - 1) // 2
    source_of, taker = sizes[1:1 + 2 * twos:2], sizes[2:2 + 2 * twos:2]
    slack = jnp.minimum(source_of - 1, most - taker)
    shifted = jax.random.randint(jax.random.fold_in(stream_key, 1), (twos,), 0, 1 << 20) % (slack + 1)
    sizes = sizes.at[1:1 + 2 * twos:2].set(source_of - shifted).at[2:2 + 2 * twos:2].set(taker + shifted)
    return sizes[jax.random.permutation(jax.random.fold_in(stream_key, 2), number_of)]


def setup_inputs(seed: int = 0) -> dict:
    key_of = jax.random.split(jax.random.key(seed), 8)
    hidden = draw_hidden(jax.random.fold_in(key_of[7], 71), 0)
    norm_gain = jnp.clip(1.0 + 0.18 * jax.random.normal(key_of[1], (D,), jnp.float32), 0.1, 1.9)
    head_weight = draw_head_weight(jax.random.fold_in(key_of[7], 71), 0)
    targets = plant(ranked(key_of[3], (TOKENS,), V, 2), jax.random.fold_in(key_of[3], 3), 0, V - 1).astype(jnp.int32)
    lengths = ragged(key_of[4], TURNS, LIVE_TOTAL, TOK_DEV, 2).astype(jnp.int32)
    prior_device = jax.random.permutation(key_of[5], TURNS).astype(jnp.int32)
    prior_row = plant(jax.random.randint(key_of[6], (TURNS,), 0, TOK_DEV), jax.random.fold_in(key_of[6], 1), 0, TOK_DEV - 1).astype(jnp.int32)
    return dict(hidden=hidden, norm_gain=norm_gain, head_weight=head_weight, targets=targets, lengths=lengths, prior_device=prior_device, prior_row=prior_row)


epsilon = 1e-05

def reference(hidden, norm_gain, head_weight, targets, lengths, prior_device, prior_row):
    blocks = hidden.reshape(TURNS, TOK_DEV, D)
    prior = blocks[prior_device, prior_row]
    scored = jnp.concatenate([prior[:, None, :], blocks[:, :-1, :]], axis=1).astype(jnp.float32)
    normed = (scored * lax.rsqrt(lax.optimization_barrier(jnp.mean(scored * scored, axis=2, keepdims=True)) + epsilon) * norm_gain.astype(jnp.float32)).astype(jnp.bfloat16)
    target_rows = targets.reshape(TURNS, TOK_DEV)

    def score(inputs):
        states, wanted = inputs
        logits = jnp.dot(states, head_weight, preferred_element_type=jnp.float32)
        largest = lax.optimization_barrier(jnp.max(logits, axis=1))
        weights = jnp.exp(logits - largest[:, None])
        totals = lax.optimization_barrier(jnp.sum(weights, axis=1))
        moments = lax.optimization_barrier(jnp.sum(weights * logits, axis=1))
        picked = jnp.take_along_axis(logits, wanted[:, None], axis=1)[:, 0]
        normalizer = largest + jnp.log(totals)
        return (picked - normalizer, normalizer - moments / totals)
    logprob, entropy = lax.map(score, (normed, target_rows))
    valid = jnp.arange(TOK_DEV, dtype=jnp.int32)[None, :] < lengths[:, None]
    logprob = jnp.where(valid, logprob, 0.0).reshape(TOKENS)
    entropy = jnp.where(valid, entropy, 0.0).reshape(TOKENS)
    return (logprob, entropy)
```

```python
import jax
import jax.numpy as jnp
from jax import lax
from jax.experimental import pallas as pl
from jax.experimental.pallas import tpu as pltpu
from jax.sharding import PartitionSpec as P

epsilon = 1e-05
MESH = pl.DeviceIdType.MESH
NZ, NY, NX, NC = 8, 4, 4, 2
OFF = (0, -1, 1, -2, 2, -3, 3, 4)
MIRROR = (0, 2, 1, 4, 3, 6, 5, 7)
HALF, PIECE = 64, 32
LOWEST = -1e30


def message_numbers():
    names = ["own_s", "own_r0", "own_r1", "own_l0", "own_l1", "fwd_r", "fwd_l"]
    names += ["share_l0", "share_l1", "share_r0", "share_r1", "share_f0", "share_f1"]
    names += [("z", side, k, p) for side in "rl" for k in range(4) for p in range(2)]
    names += [("x", s, p) for s in range(1, NZ) for p in range(2)]
    names += [("target", s) for s in range(1, NZ)]
    names += [("row_y", d) for d in range(1, NY)]
    names += [("row_z", s) for s in range(1, NZ)]
    names += [("stat_z", s) for s in range(1, NZ)]
    names += [("stat_v", i, j) for i in range(NX) for j in range(NC) if i + j]
    return {name: at for at, name in enumerate(names)}


NUMBER = message_numbers()


def peer(dx=0, dy=0, dz=0, dc=0):
    tok, voc = lax.axis_index("tok"), lax.axis_index("voc")
    z, y, x, c = tok // NY, tok % NY, voc // NC, voc % NC
    return (
        ((z + dz + NZ) % NZ) * NY + (y + dy + NY) % NY,
        ((x + dx + NX) % NX) * NC + (c + dc) % NC,
    )


PEERS = (
    [dict(dy=d) for d in range(1, NY)]
    + [dict(dz=d) for d in range(1, NZ)]
    + [dict(dx=i, dc=j) for i in range(NX) for j in range(NC) if i + j]
)


def kernel(
    lengths, prior_device, prior_row, hidden, gain, weight, targets,
    logprob, entropy,
    wbuf, tbuf, gbuf, tgt, row_y, row_z, prior, stats, mine_z, got_z, mine_v, got_v,
    send, recv, local,
):
    tok, voc = lax.axis_index("tok"), lax.axis_index("voc")
    z, y, x, c = tok // NY, tok % NY, voc // NC, voc % NC
    kind = x % 2
    width = weight.shape[0]
    half = width // 2
    wide = 2 * width

    barrier = pltpu.get_barrier_semaphore()
    for offsets in PEERS:
        pl.semaphore_signal(barrier, inc=1, device_id=peer(**offsets), device_id_type=MESH)

    fetch = pltpu.make_async_copy(weight, wbuf.at[pl.ds(0, width)], local)
    fetch.start()

    def copy(name, source, target, **offsets):
        at = NUMBER[name]
        return pltpu.make_async_remote_copy(
            src_ref=source, dst_ref=target, send_sem=send.at[at], recv_sem=recv.at[at],
            device_id=peer(**offsets), device_id_type=MESH,
        )

    def wrows(start, rows):
        return wbuf.at[pl.ds(start, rows)]

    left, right, far = wide, 2 * wide, 3 * wide
    weight_messages = {
        "own_s": (0, width, width, dict(dc=1)),
        "own_r0": (0, left, half, dict(dy=1)),
        "own_r1": (half, left + half, half, dict(dy=1)),
        "own_l0": (0, right, half, dict(dy=-1)),
        "own_l1": (half, right + half, half, dict(dy=-1)),
        "fwd_r": (left, far, half, dict(dy=1)),
        "fwd_l": (right + half, far + half, half, dict(dy=-1)),
        "share_l0": (left, left + width, half, dict(dc=1)),
        "share_l1": (left + half, left + width + half, half, dict(dc=1)),
        "share_r0": (right, right + width, half, dict(dc=1)),
        "share_r1": (right + half, right + width + half, half, dict(dc=1)),
        "share_f0": (far, far + width, half, dict(dc=1)),
        "share_f1": (far + half, far + width + half, half, dict(dc=1)),
    }

    def weights(name):
        source, target, rows, offsets = weight_messages[name]
        return copy(name, wrows(source, rows), wrows(target, rows), **offsets)

    def trows(slot, which, p):
        start = pl.multiple_of(slot * 2 * HALF + which * HALF + p * PIECE, PIECE)
        return tbuf.at[pl.ds(start, PIECE)]

    source_slot = {"r": (0, 1, 3, 5), "l": (0, 2, 4, 6)}
    target_slot = {"r": (1, 3, 5, 7), "l": (2, 4, 6, 7)}

    def along_z(side, k, p):
        return copy(
            ("z", side, k, p),
            trows(source_slot[side][k], kind, p),
            trows(target_slot[side][k], kind, p),
            dz=1 if side == "r" else -1,
        )

    def along_x(s, p):
        return copy(("x", s, p), trows(s, kind, p), trows(s, kind, p), dx=1 if p == 0 else -1)

    def from_x(s, p):
        return copy(("x", s, p), trows(s, 1 - kind, p), trows(s, 1 - kind, p), dx=1 if p == 0 else -1)

    def target_message(s):
        return copy(("target", s), tgt.at[0], tgt.at[MIRROR[s]], dz=OFF[s])

    def target_arrival(s):
        return copy(("target", s), tgt.at[MIRROR[s]], tgt.at[MIRROR[s]], dz=OFF[s])

    def row_y_message(d):
        return copy(("row_y", d), row_y.at[0], row_y.at[d], dy=d)

    def row_z_message(s):
        return copy(("row_z", s), row_z.at[z], row_z.at[z], dz=OFF[s])

    def row_z_arrival(s):
        origin = (z - OFF[s] + NZ) % NZ
        return copy(("row_z", s), row_z.at[origin], row_z.at[origin], dz=OFF[s])

    def stat_z_message(s):
        return copy(("stat_z", s), mine_z.at[s], got_z.at[MIRROR[s]], dz=OFF[s])

    def stat_v_message(i, j):
        return copy(("stat_v", i, j), mine_v, got_v.at[voc], dx=i, dc=j)

    def stat_v_arrival(i, j):
        origin = ((x - i + NX) % NX) * NC + (c + j) % NC
        return copy(("stat_v", i, j), got_v.at[origin], got_v.at[origin], dx=i, dc=j)

    sent = []

    def start(make, *which):
        make(*which).start()
        sent.append((make, which))

    def norm(rows):
        mean = jnp.sum(rows * rows, axis=1, keepdims=True) / rows.shape[1]
        return rows * lax.rsqrt(mean + epsilon) * gain[...]

    mine = hidden[pl.ds(pl.multiple_of(c * 2 * HALF, 2 * HALF), 2 * HALF), :].astype(jnp.float32)
    tbuf[pl.ds(0, 2 * HALF), :] = norm(mine).astype(jnp.bfloat16)
    asked = jnp.int32(0)
    for t in range(NZ * NY):
        asked = asked + jnp.where(prior_device[t] == tok, prior_row[t], 0)
    shape = (8, hidden.shape[0])
    chosen = (lax.broadcasted_iota(jnp.int32, shape, 0) == y) & (lax.broadcasted_iota(jnp.int32, shape, 1) == asked)
    outgoing = jnp.dot(
        jnp.where(chosen, 1.0, 0.0).astype(jnp.bfloat16), hidden[...], preferred_element_type=jnp.float32
    )
    row_y[0] = norm(outgoing).astype(jnp.bfloat16)
    shifted = pltpu.roll(jnp.broadcast_to(targets[...], shape), shape[1] - 1, 1)
    tgt[0] = jnp.where(c == 0, shifted[:, : 2 * HALF], shifted[:, 2 * HALF :])
    prior[...] = jnp.zeros_like(prior)
    for g in range(4):
        stats[g, 0] = jnp.full(stats.shape[2:], LOWEST, jnp.float32)
        for k in range(1, 4):
            stats[g, k] = jnp.zeros(stats.shape[2:], jnp.float32)

    pl.semaphore_wait(barrier, len(PEERS))

    for d in range(1, NY):
        start(row_y_message, d)
    for p in range(2):
        start(along_z, "r", 0, p)
        start(along_z, "l", 0, 1 - p)
    fetch.wait()
    for name in ("own_r0", "own_l1", "own_r1", "own_l0", "own_s"):
        start(weights, name)
    for s in range(1, NZ):
        start(target_message, s)

    for d in range(1, NY):
        row_y_message(d).wait_recv()
    gathered = row_y[0].astype(jnp.float32)
    for d in range(1, NY):
        gathered = gathered + row_y[d].astype(jnp.float32)

    @pl.when(c == 1)
    def _():
        row_z[z] = gathered.astype(jnp.bfloat16)
        for s in range(1, NZ):
            row_z_message(s).start()

    def pass_on(k, late):
        for side in "rl":
            p = late if side == "r" else 1 - late
            slot = target_slot[side][k]
            along_z(side, k, p).wait_recv()
            if k < 2 or (k == 2 and late == 0):
                start(along_z, side, k + 1, p)
            start(along_x, slot, p)

    def whole(slot):
        for p in range(2):
            from_x(slot, p).wait_recv()

    def assemble(slots):
        for s in slots:
            low = s * 2 * HALF
            gbuf[low : low + 2 * HALF - 16] = tbuf[low : low + 2 * HALF - 16]
            last = tbuf[low + 2 * HALF - 16 : low + 2 * HALF].astype(jnp.float32)
            here = (lax.broadcasted_iota(jnp.int32, last.shape, 0) == 15) & (c == 1)
            last = jnp.where(here, jnp.broadcast_to(prior[s : s + 1, :], last.shape), last)
            gbuf[low + 2 * HALF - 16 : low + 2 * HALF] = last.astype(jnp.bfloat16)

    def unit(g, d):
        rows = 4 * HALF
        w = wbuf[pl.ds(pl.multiple_of(d * wide, wide), wide), :]
        t = gbuf[pl.ds(pl.multiple_of(g * rows, rows), rows), :]
        logits = lax.dot_general(w, t, (((1,), (1,)), ((), ())), preferred_element_type=jnp.float32)
        logits = logits.reshape(wide // 8, 8, rows)
        old = stats[g, 0]
        top = jnp.maximum(old, jnp.max(logits, axis=0))
        scale = jnp.exp(old - top)
        e = jnp.exp(logits - top[None])
        stats[g, 0] = top
        stats[g, 1] = stats[g, 1] * scale + jnp.sum(e, axis=0)
        stats[g, 2] = stats[g, 2] * scale + jnp.sum(e * logits, axis=0)
        y_of = (y + jnp.where(d == 1, 3, jnp.where(d == 2, 1, jnp.where(d == 3, 2, 0)))) % NY
        wanted = jnp.concatenate([tgt[2 * g], tgt[2 * g + 1]], axis=1) - lax.broadcasted_iota(jnp.int32, (8, rows), 0)
        picked = stats[g, 3]
        each = width // 8
        for s in range(NC):
            base = ((z * NY + y_of) * (NX * NC) + x * NC + (c + s) % NC) * width
            at = lax.broadcasted_iota(jnp.int32, (each, 8, rows), 0) * 8
            hit = at == (wanted - base)[None]
            picked = picked + jnp.sum(jnp.where(hit, logits[s * each : (s + 1) * each], 0.0), axis=0)
        stats[g, 3] = picked

    def first_units(k, carry):
        @pl.when(k == 0)
        def _():
            pass_on(0, 0)
            pass_on(0, 1)
            weights("own_r0").wait_recv()
            start(weights, "fwd_r")
            start(weights, "share_l0")
            weights("own_l1").wait_recv()
            start(weights, "fwd_l")
            start(weights, "share_r1")
            pass_on(1, 0)
            pass_on(1, 1)
            weights("own_s").wait_recv()
            for s in range(1, NZ):
                target_arrival(s).wait_recv()

            @pl.when(c == 1)
            def _():
                for s in range(1, NZ):
                    row_z_arrival(s).wait_recv()
                shape = (8, NZ * 8)
                wants = jnp.full(shape, -1, jnp.int32)
                sub = lax.broadcasted_iota(jnp.int32, shape, 0)
                for s in range(NZ):
                    turn = ((z + OFF[s] + NZ) % NZ) * NY + y
                    wants = jnp.where(sub == s, prior_device[turn], wants)
                lane = lax.broadcasted_iota(jnp.int32, shape, 1)
                block = jnp.where(lane % 8 < NY, lane // 8 * NY + lane % 8, -2)
                pick = jnp.where(wants == block, 1.0, 0.0).astype(jnp.bfloat16)
                table = row_z[...].reshape(NZ * 8, row_z.shape[2])
                prior[...] = jnp.dot(pick, table, preferred_element_type=jnp.float32)

            whole(1)
            assemble((0, 1))

        @pl.when(k == 1)
        def _():
            pass_on(2, 0)
            weights("own_r1").wait_recv()
            start(weights, "share_l1")
            weights("own_l0").wait_recv()
            start(weights, "share_r0")
            pass_on(2, 1)
            for name in ("share_l0", "share_l1", "share_r0", "share_r1"):
                weights(name).wait_recv()

        @pl.when(k == 3)
        def _():
            whole(2)
            whole(3)
            assemble((2, 3))

        @pl.when(k == 6)
        def _():
            along_z("r", 3, 0).wait_recv()
            start(along_x, 7, 0)
            along_z("l", 3, 1).wait_recv()
            start(along_x, 7, 1)
            whole(4)
            whole(5)
            assemble((4, 5))

        @pl.when(k == 9)
        def _():
            weights("fwd_r").wait_recv()
            start(weights, "share_f0")
            weights("fwd_l").wait_recv()
            start(weights, "share_f1")
            whole(6)
            whole(7)
            assemble((6, 7))

        @pl.when(k == 12)
        def _():
            weights("share_f0").wait_recv()
            weights("share_f1").wait_recv()

        unit(jnp.where(k < 12, k // 3, k - 12), jnp.where(k < 12, k % 3, 3))
        return carry

    lax.fori_loop(0, 16, first_units, 0)

    sub = lax.broadcasted_iota(jnp.int32, (8, 2 * HALF), 0)

    def tile(top, total, moment, picked):
        return jnp.where(sub == 0, top, jnp.where(sub == 1, total, jnp.where(sub == 2, moment, picked)))

    for s in range(NZ):
        lanes = slice(s % 2 * 2 * HALF, (s % 2 + 1) * 2 * HALF)
        tops = stats[s // 2, 0, :, lanes]
        top = jnp.max(tops, axis=0, keepdims=True)
        scale = jnp.exp(tops - top)
        total = jnp.sum(stats[s // 2, 1, :, lanes] * scale, axis=0, keepdims=True)
        moment = jnp.sum(stats[s // 2, 2, :, lanes] * scale, axis=0, keepdims=True)
        picked = jnp.sum(stats[s // 2, 3, :, lanes], axis=0, keepdims=True)
        mine_z[s] = tile(top, total, moment, picked)
        if s:
            start(stat_z_message, s)

    def merge(tiles):
        top = tiles[0][0:1]
        for other in tiles[1:]:
            top = jnp.maximum(top, other[0:1])
        total, moment, picked = 0.0, 0.0, 0.0
        for one in tiles:
            scale = jnp.exp(one[0:1] - top)
            total = total + one[1:2] * scale
            moment = moment + one[2:3] * scale
            picked = picked + one[3:4]
        return top, total, moment, picked

    for s in range(1, NZ):
        copy(("stat_z", s), mine_z.at[s], got_z.at[MIRROR[s]], dz=OFF[s]).wait_recv()
    merged = tile(*merge([mine_z[0]] + [got_z[s] for s in range(1, NZ)]))
    mine_v[...] = merged
    for i in range(NX):
        for j in range(NC):
            if i + j:
                start(stat_v_message, i, j)
    got_v[voc] = merged
    for i in range(NX):
        for j in range(NC):
            if i + j:
                stat_v_arrival(i, j).wait_recv()
    row_of, entropy_of = [], []
    for h in range(NC):
        top, total, moment, picked = merge([got_v[i * NC + h] for i in range(NX)])
        normalizer = top + jnp.log(total)
        row_of.append(picked - normalizer)
        entropy_of.append(normalizer - moment / total)
    live = lax.broadcasted_iota(jnp.int32, (1, 4 * HALF), 1) < lengths[tok]

    def finished(parts):
        both = jnp.broadcast_to(jnp.concatenate(parts, axis=1), (8, 4 * HALF))
        return jnp.where(live, pltpu.roll(both, 1, 1)[0:1], 0.0)

    logprob[...] = finished(row_of)
    entropy[...] = finished(entropy_of)

    for make, which in sent:
        make(*which).wait_send()

    @pl.when(c == 1)
    def _():
        for s in range(1, NZ):
            row_z_message(s).wait_send()


def body(hidden, norm_gain, head_weight, targets, lengths, prior_device, prior_row):
    rows, features = hidden.shape
    width = head_weight.shape[1]
    vmem, smem = pl.BlockSpec(memory_space=pltpu.VMEM), pl.BlockSpec(memory_space=pltpu.SMEM)
    f32, bf16 = jnp.float32, jnp.bfloat16
    out = jax.ShapeDtypeStruct((1, rows), f32)
    lanes = 2 * HALF
    logprob, entropy = pl.pallas_call(
        kernel,
        out_shape=(out, out),
        in_specs=[smem, smem, smem, vmem, vmem, pl.BlockSpec(memory_space=pl.ANY), vmem],
        out_specs=(vmem, vmem),
        scratch_shapes=[
            pltpu.VMEM((8 * width, features), bf16),
            pltpu.VMEM((NZ * lanes, features), bf16),
            pltpu.VMEM((NZ * lanes, features), bf16),
            pltpu.VMEM((NZ, 8, lanes), jnp.int32),
            pltpu.VMEM((NY, 8, features), bf16),
            pltpu.VMEM((NZ, 8, features), bf16),
            pltpu.VMEM((8, features), f32),
            pltpu.VMEM((4, 4, 8, 2 * lanes), f32),
            pltpu.VMEM((NZ, 8, lanes), f32),
            pltpu.VMEM((NZ, 8, lanes), f32),
            pltpu.VMEM((8, lanes), f32),
            pltpu.VMEM((NX * NC, 8, lanes), f32),
            pltpu.SemaphoreType.DMA((len(NUMBER),)),
            pltpu.SemaphoreType.DMA((len(NUMBER),)),
            pltpu.SemaphoreType.DMA,
        ],
        compiler_params=pltpu.CompilerParams(
            collective_id=0, has_side_effects=True, vmem_limit_bytes=48 * 2**20
        ),
    )(
        lengths, prior_device, prior_row, hidden, norm_gain.reshape(1, features), head_weight.T,
        targets.reshape(1, rows),
    )
    return logprob.reshape(rows), entropy.reshape(rows)


def solution(mesh):
    in_specs = (P("tok", None), P(), P(None, ("tok", "voc")), P("tok"), P(), P(), P())
    out_specs = (P("tok"), P("tok"))
    return jax.shard_map(body, mesh=mesh, in_specs=in_specs, out_specs=out_specs, check_vma=False)
```

```python
import jax
import jax.numpy as jnp
from jax import lax
from jax.experimental import pallas as pl
from jax.experimental.pallas import tpu as pltpu
from jax.sharding import PartitionSpec as P

epsilon = 1e-05
MESH = pl.DeviceIdType.MESH
NZ, NY, NX, NC = 8, 4, 4, 2
OFF = (0, -1, 1, -2, 2, -3, 3, 4)
MIRROR = (0, 2, 1, 4, 3, 6, 5, 7)
HALF, PIECE = 64, 32
KEPT = (None, 128, 192, 384, 448, 640, 704, 896)
SWAPPED = (None, 256, 320, 512, 576, 768, 832, 960)
LOWEST = -1e30


def message_numbers():
    names = ["own_s"] + [(side, part) for side in "rl" for part in ("a", "b", "f0", "f1", "f2")]
    names += [("share", d, q) for d in range(1, 3) for q in (0, 2)]
    names += [("share", 3, q, step) for q in (0, 2) for step in range(3)]
    names += [("z", side, k, p) for side in "rl" for k in range(4) for p in range(2)]
    names += [("x", s, p) for s in range(1, NZ) for p in range(2)]
    names += [("target", s) for s in range(1, NZ)]
    names += [("row_y", d) for d in range(1, NY)]
    names += [("row_z", s) for s in range(1, NZ)]
    names += [("stat_z", s) for s in range(1, NZ)]
    names += [("stat_v", i, j) for i in range(NX) for j in range(NC) if i + j]
    return {name: at for at, name in enumerate(names)}


NUMBER = message_numbers()


def peer(dx=0, dy=0, dz=0, dc=0):
    tok, voc = lax.axis_index("tok"), lax.axis_index("voc")
    z, y, x, c = tok // NY, tok % NY, voc // NC, voc % NC
    return (
        ((z + dz + NZ) % NZ) * NY + (y + dy + NY) % NY,
        ((x + dx + NX) % NX) * NC + (c + dc) % NC,
    )


PEERS = [dict(dx=1), dict(dx=-1), dict(dz=1), dict(dz=-1), dict(dc=1)] + [dict(dy=d) for d in range(1, NY)]
RELAYS = 4


def kernel(
    lengths_hbm, device_hbm, row_hbm, hidden_hbm, gain_hbm, weight, targets_hbm,
    logprob, entropy,
    lengths, prior_device, prior_row, hidden, gain, targets,
    wbuf, tbuf, gbuf, tgt, wanted, row_y, row_z, prior, stats, mine_z, got_z, mine_v, got_v,
    send, recv, local, relay,
):
    tok, voc = lax.axis_index("tok"), lax.axis_index("voc")
    z, y, x, c = tok // NY, tok % NY, voc // NC, voc % NC
    kind = x % 2
    width = weight.shape[0]
    half = width // 2
    third = half // 3
    wide = 2 * width
    block = 2 * HALF

    own_rows = pl.ds(pl.multiple_of(c * block, block), block)
    other_rows = pl.ds(pl.multiple_of((1 - c) * block, block), block)
    fetches = [
        pltpu.make_async_copy(weight, wbuf.at[pl.ds(0, width)], local.at[0]),
        pltpu.make_async_copy(hidden_hbm.at[own_rows], hidden.at[own_rows], local.at[1]),
        pltpu.make_async_copy(gain_hbm, gain, local.at[2]),
        pltpu.make_async_copy(hidden_hbm.at[other_rows], hidden.at[other_rows], local.at[3]),
        pltpu.make_async_copy(device_hbm, prior_device, local.at[4]),
        pltpu.make_async_copy(row_hbm, prior_row, local.at[5]),
        pltpu.make_async_copy(targets_hbm, targets, local.at[6]),
        pltpu.make_async_copy(lengths_hbm, lengths, local.at[7]),
    ]
    barrier = pltpu.get_barrier_semaphore()
    for offsets in PEERS:
        pl.semaphore_signal(barrier, inc=1, device_id=peer(**offsets), device_id_type=MESH)
    for fetch in fetches:
        fetch.start()

    def copy(name, source, target, **offsets):
        at = NUMBER[name]
        return pltpu.make_async_remote_copy(
            src_ref=source, dst_ref=target, send_sem=send.at[at], recv_sem=recv.at[at],
            device_id=peer(**offsets), device_id_type=MESH,
        )

    def part_row(d, q):
        return d * wide + q * half

    def weights(name):
        if name == "own_s":
            source, target, rows, offsets = 0, width, width, dict(dc=1)
        elif name[0] == "share" and name[1] == 3:
            step = name[3] * third
            source, target, rows = part_row(3, name[2]) + step, part_row(3, name[2] + 1) + step, third
            offsets = dict(dc=1)
        elif name[0] == "share":
            source, target, rows = part_row(name[1], name[2]), part_row(name[1], name[2] + 1), half
            offsets = dict(dc=1)
        else:
            side, part = name
            q, offsets = (0, dict(dy=1)) if side == "r" else (2, dict(dy=-1))
            first = 0 if side == "r" else half
            if part == "b":
                source, target, rows = half - first, part_row(2, q), half
            elif part == "a":
                source, target, rows = first, part_row(1, q), half
            else:
                step = int(part[1]) * third
                source, target, rows = part_row(1, q) + step, part_row(3, q) + step, third
        return copy(name, wbuf.at[pl.ds(source, rows)], wbuf.at[pl.ds(target, rows)], **offsets)

    source_slot = {"r": (0, 1, 3, 5), "l": (0, 2, 4, 6)}
    target_slot = {"r": (1, 3, 5, 7), "l": (2, 4, 6, 7)}

    def piece(start, p):
        return tbuf.at[pl.ds(start + p * PIECE, PIECE)]

    def along_z(side, k, p):
        if k:
            source = piece(KEPT[source_slot[side][k]], p)
        else:
            source = tbuf.at[pl.ds(pl.multiple_of(kind * HALF + p * PIECE, PIECE), PIECE)]
        return copy(
            ("z", side, k, p), source, piece(KEPT[target_slot[side][k]], p), dz=1 if side == "r" else -1
        )

    def along_x(s, p):
        return copy(("x", s, p), piece(KEPT[s], p), piece(SWAPPED[s], p), dx=1 if p == 0 else -1)

    def target_message(s):
        return copy(("target", s), tgt.at[0], tgt.at[MIRROR[s]], dz=OFF[s])

    def row_y_message(d):
        return copy(("row_y", d), row_y.at[0], row_y.at[d], dy=d)

    def row_z_message(s):
        return copy(("row_z", s), row_z.at[z], row_z.at[z], dz=OFF[s])

    def row_z_arrival(s):
        origin = (z - OFF[s] + NZ) % NZ
        return copy(("row_z", s), row_z.at[origin], row_z.at[origin], dz=OFF[s])

    def stat_z_message(s):
        return copy(("stat_z", s), mine_z.at[s], got_z.at[MIRROR[s]], dz=OFF[s])

    def stat_v_message(i, j):
        return copy(("stat_v", i, j), mine_v, got_v.at[voc], dx=i, dc=j)

    def stat_v_arrival(i, j):
        origin = ((x - i + NX) % NX) * NC + (c + j) % NC
        return copy(("stat_v", i, j), got_v.at[origin], got_v.at[origin], dx=i, dc=j)

    sent = []

    def start(make, *which):
        make(*which).start()
        sent.append((make, which))

    def norm(rows):
        mean = jnp.sum(rows * rows, axis=1, keepdims=True) / rows.shape[1]
        return rows * lax.rsqrt(mean + epsilon) * gain[...]

    def norm_half(which):
        low = pl.multiple_of(c * block + which * HALF, HALF)
        rows = norm(hidden[pl.ds(low, HALF), :].astype(jnp.float32))
        tbuf[pl.ds(pl.multiple_of(which * HALF, HALF), HALF), :] = rows.astype(jnp.bfloat16)

    for fetch in fetches[1:]:
        fetch.wait()
    norm_half(kind)
    asked = jnp.int32(0)
    for t in range(NZ * NY):
        asked = asked + jnp.where(prior_device[t] == tok, prior_row[t], 0)
    shape = (8, hidden.shape[0])
    chosen = (lax.broadcasted_iota(jnp.int32, shape, 0) == y) & (lax.broadcasted_iota(jnp.int32, shape, 1) == asked)
    outgoing = jnp.dot(
        jnp.where(chosen, 1.0, 0.0).astype(jnp.bfloat16), hidden[...], preferred_element_type=jnp.float32
    )
    row_y[0] = norm(outgoing).astype(jnp.bfloat16)
    fetches[0].wait()

    pl.semaphore_wait(barrier, len(PEERS))
    for d in range(1, NY):
        start(row_y_message, d)
    for p in range(2):
        start(along_z, "r", 0, p)
        start(along_z, "l", 0, 1 - p)
    for part in "ab":
        for side in "rl":
            start(weights, (side, part))
    start(weights, "own_s")

    def tell(level, axis):
        for d in (1, -1):
            pl.semaphore_signal(relay.at[level], inc=1, device_id=peer(**{axis: d}), device_id_type=MESH)

    tell(0, "dz")
    tell(3, "dx")

    def turned(value):
        return jnp.where(kind == 0, value, pltpu.roll(value, HALF, 1))

    shifted = pltpu.roll(jnp.broadcast_to(targets[...], shape), shape[1] - 1, 1)
    straight = jnp.where(c == 0, shifted[:, :block], shifted[:, block:])
    tgt[0] = turned(straight)
    pl.semaphore_wait(relay.at[0], 2)
    tell(1, "dz")
    norm_half(1 - kind)
    prior[...] = jnp.zeros_like(prior)
    for g in range(4):
        stats[g, 0] = jnp.full(stats.shape[2:], LOWEST, jnp.float32)
        for k in range(1, 4):
            stats[g, k] = jnp.zeros(stats.shape[2:], jnp.float32)
    pl.semaphore_wait(relay.at[1], 2)
    tell(2, "dz")
    pl.semaphore_wait(relay.at[3], 2)
    for d in range(1, NY):
        row_y_message(d).wait_recv()
    gathered = row_y[0].astype(jnp.float32)
    for d in range(1, NY):
        gathered = gathered + row_y[d].astype(jnp.float32)
    pl.semaphore_wait(relay.at[2], 2)

    @pl.when(c == 1)
    def _():
        row_z[z] = gathered[:NY].astype(jnp.bfloat16)
        for s in range(1, NZ):
            row_z_message(s).start()

    for s in range(1, NZ):
        start(target_message, s)

    def pass_on(k, late):
        for side in "rl":
            p = late if side == "r" else 1 - late
            along_z(side, k, p).wait_recv()
            if k < 2 or (k == 2 and late == 0):
                start(along_z, side, k + 1, p)
            start(along_x, target_slot[side][k], p)

    def whole(slot):
        for p in range(2):
            along_x(slot, p).wait_recv()

    def assemble(g):
        rows = 2 * block
        gbuf[g * rows : (g + 1) * rows] = tbuf[g * rows : (g + 1) * rows]
        tails = [(HALF, 0, 1)] if g == 0 else []
        tails += [(KEPT[s], s, kind) for s in range(1, NZ)] + [(SWAPPED[s], s, 1 - kind) for s in range(1, NZ)]
        for low, s, which in tails:
            if low // rows == g:
                last = tbuf[low + HALF - 16 : low + HALF].astype(jnp.float32)
                here = (lax.broadcasted_iota(jnp.int32, last.shape, 0) == 15) & (c * which == 1)
                last = jnp.where(here, jnp.broadcast_to(prior[s : s + 1, :], last.shape), last)
                gbuf[low + HALF - 16 : low + HALF] = last.astype(jnp.bfloat16)

    lane = lax.broadcasted_iota(jnp.int32, (8, block), 1)

    def kept_pair(first, second):
        return jnp.where(lane < HALF, first, pltpu.roll(second, HALF, 1))

    def swapped_pair(first, second):
        return jnp.where(lane < HALF, pltpu.roll(first, HALF, 1), second)

    def unit(g, d):
        rows = 2 * block
        w = wbuf[pl.ds(pl.multiple_of(d * wide, wide), wide), :]
        t = gbuf[pl.ds(pl.multiple_of(g * rows, rows), rows), :]
        logits = lax.dot_general(w, t, (((1,), (1,)), ((), ())), preferred_element_type=jnp.float32)
        logits = logits.reshape(wide // 8, 8, rows)
        old = stats[g, 0]
        top = jnp.maximum(old, jnp.max(logits, axis=0))
        scale = jnp.exp(old - top)
        e = jnp.exp(logits - top[None])
        stats[g, 0] = top
        stats[g, 1] = stats[g, 1] * scale + jnp.sum(e, axis=0)
        stats[g, 2] = stats[g, 2] * scale + jnp.sum(e * logits, axis=0)
        picked = stats[g, 3]
        each = half // 8
        for q in range(4):
            side = jnp.where(d == 0, 0, jnp.where(d == 3, 2, 3 if q < 2 else 1))
            core = jnp.where(d == 0, q // 2, q % 2)
            part = jnp.where(d == 0, q % 2, jnp.where(d == 2, 1 - q // 2, q // 2))
            device = (z * NY + (y + side) % NY) * (NX * NC) + x * NC + (c + core) % NC
            at = lax.broadcasted_iota(jnp.int32, (each, 8, rows), 0) * 8
            hit = at == (wanted[g] - (device * width + part * half))[None]
            picked = picked + jnp.sum(jnp.where(hit, logits[q * each : (q + 1) * each], 0.0), axis=0)
        stats[g, 3] = picked

    sub = lax.broadcasted_iota(jnp.int32, (8, block), 0)

    def tile(top, total, moment, picked):
        return jnp.where(sub == 0, top, jnp.where(sub == 1, total, jnp.where(sub == 2, moment, picked)))

    def reduced(g, which):
        lanes = slice(which * block, (which + 1) * block)
        tops = stats[g, 0, :, lanes]
        top = jnp.max(tops, axis=0, keepdims=True)
        scale = jnp.exp(tops - top)
        return tile(
            top,
            jnp.sum(stats[g, 1, :, lanes] * scale, axis=0, keepdims=True),
            jnp.sum(stats[g, 2, :, lanes] * scale, axis=0, keepdims=True),
            jnp.sum(stats[g, 3, :, lanes], axis=0, keepdims=True),
        )

    def give_pair(g):
        kept, swapped = reduced(g, 1), reduced(g + 1, 0)
        mine_z[2 * g + 1] = kept_pair(kept, swapped)
        mine_z[2 * g + 2] = jnp.where(lane < HALF, pltpu.roll(kept, HALF, 1), swapped)

    def units(k, carry):
        @pl.when(k == 0)
        def _():
            pass_on(0, 0)
            pass_on(0, 1)
            for q, side in ((0, "r"), (2, "l")):
                weights((side, "a")).wait_recv()
                for step in range(3):
                    start(weights, (side, f"f{step}"))
                start(weights, ("share", 1, q))
            pass_on(1, 0)
            pass_on(1, 1)
            weights("own_s").wait_recv()
            for s in range(1, NZ):
                target_message(s).wait_recv()
            pairs = [(s, s + 1) for s in (1, 3, 5)]
            kept = [kept_pair(tgt[i], tgt[j]) for i, j in pairs]
            swapped = [swapped_pair(tgt[i], tgt[j]) for i, j in pairs]
            for g, both in enumerate(zip([straight] + swapped, kept + [tgt[7]])):
                place = lax.broadcasted_iota(jnp.int32, (8, 2 * block), 0)
                wanted[g] = jnp.concatenate(both, axis=1) - place

            @pl.when(c == 1)
            def _():
                for s in range(1, NZ):
                    row_z_arrival(s).wait_recv()
                shape = (8, NZ * NY)
                wants = jnp.full(shape, -1, jnp.int32)
                place = lax.broadcasted_iota(jnp.int32, shape, 0)
                for s in range(NZ):
                    turn = ((z + OFF[s] + NZ) % NZ) * NY + y
                    wants = jnp.where(place == s, prior_device[turn], wants)
                across = lax.broadcasted_iota(jnp.int32, shape, 1)
                pick = jnp.where(wants == across, 1.0, 0.0).astype(jnp.bfloat16)
                table = row_z[...].reshape(NZ * NY, row_z.shape[2])
                prior[...] = jnp.dot(pick, table, preferred_element_type=jnp.float32)

            whole(1)
            whole(2)
            assemble(0)
            assemble(1)

        @pl.when(k == 2)
        def _():
            pass_on(2, 0)
            weights(("share", 1, 0)).wait_recv()
            weights(("share", 1, 2)).wait_recv()

        @pl.when(k == 4)
        def _():
            pass_on(2, 1)
            for q, side in ((0, "r"), (2, "l")):
                weights((side, "b")).wait_recv()
                start(weights, ("share", 2, q))
            whole(3)
            whole(4)
            assemble(2)

        def share_far(step):
            for q, side in ((0, "r"), (2, "l")):
                weights((side, f"f{step}")).wait_recv()
                start(weights, ("share", 3, q, step))

        @pl.when(k == 6)
        def _():
            along_z("r", 3, 0).wait_recv()
            start(along_x, 7, 0)
            along_z("l", 3, 1).wait_recv()
            start(along_x, 7, 1)
            share_far(0)
            for q in (0, 2):
                weights(("share", 2, q)).wait_recv()

        @pl.when(k == 8)
        def _():
            share_far(1)

        @pl.when(k == 9)
        def _():
            whole(5)
            whole(6)
            whole(7)
            assemble(3)

        @pl.when(k == 10)
        def _():
            share_far(2)

        @pl.when(k == 12)
        def _():
            for q in (0, 2):
                for step in range(3):
                    weights(("share", 3, q, step)).wait_recv()

        @pl.when(k == 13)
        def _():
            mine_z[7] = reduced(3, 1)
            start(stat_z_message, 7)

        @pl.when(k == 14)
        def _():
            give_pair(2)
            start(stat_z_message, 5)
            start(stat_z_message, 6)

        @pl.when(k == 15)
        def _():
            give_pair(1)
            start(stat_z_message, 3)
            start(stat_z_message, 4)

        early = jnp.where(k < 4, k % 2, jnp.where(k < 6, 2, k - 6))
        unit(
            jnp.where(k < 9, early, jnp.where(k < 12, 3, 15 - k)),
            jnp.where(k < 4, k // 2, jnp.where(k < 6, k - 4, jnp.where(k < 9, 2, jnp.where(k < 12, k - 9, 3)))),
        )
        return carry

    lax.fori_loop(0, 16, units, 0)
    give_pair(0)
    start(stat_z_message, 1)
    start(stat_z_message, 2)
    mine_z[0] = turned(reduced(0, 0))

    def merge(tiles):
        top = tiles[0][0:1]
        for other in tiles[1:]:
            top = jnp.maximum(top, other[0:1])
        total, moment, picked = 0.0, 0.0, 0.0
        for one in tiles:
            scale = jnp.exp(one[0:1] - top)
            total = total + one[1:2] * scale
            moment = moment + one[2:3] * scale
            picked = picked + one[3:4]
        return top, total, moment, picked

    for s in range(1, NZ):
        stat_z_message(s).wait_recv()
    merged = turned(tile(*merge([mine_z[0]] + [got_z[s] for s in range(1, NZ)])))
    mine_v[...] = merged
    for i in range(NX):
        for j in range(NC):
            if i + j:
                start(stat_v_message, i, j)
    got_v[voc] = merged
    for i in range(NX):
        for j in range(NC):
            if i + j:
                stat_v_arrival(i, j).wait_recv()
    row_of, entropy_of = [], []
    for h in range(NC):
        top, total, moment, picked = merge([got_v[i * NC + h] for i in range(NX)])
        normalizer = top + jnp.log(total)
        row_of.append(picked - normalizer)
        entropy_of.append(normalizer - moment / total)
    live = lax.broadcasted_iota(jnp.int32, (1, 2 * block), 1) < lengths[tok]

    def finished(parts):
        both = jnp.broadcast_to(jnp.concatenate(parts, axis=1), (8, 2 * block))
        return jnp.where(live, pltpu.roll(both, 1, 1)[0:1], 0.0)

    logprob[...] = finished(row_of)
    entropy[...] = finished(entropy_of)

    for make, which in sent:
        make(*which).wait_send()

    @pl.when(c == 1)
    def _():
        for s in range(1, NZ):
            row_z_message(s).wait_send()


def body(hidden, norm_gain, head_weight, targets, lengths, prior_device, prior_row):
    rows, features = hidden.shape
    width = head_weight.shape[1]
    vmem, hbm = pl.BlockSpec(memory_space=pltpu.VMEM), pl.BlockSpec(memory_space=pltpu.HBM)
    f32, bf16 = jnp.float32, jnp.bfloat16
    out = jax.ShapeDtypeStruct((1, rows), f32)
    lanes = 2 * HALF
    logprob, entropy = pl.pallas_call(
        kernel,
        out_shape=(out, out),
        in_specs=[hbm] * 7,
        out_specs=(vmem, vmem),
        scratch_shapes=[
            pltpu.SMEM(lengths.shape, jnp.int32),
            pltpu.SMEM(lengths.shape, jnp.int32),
            pltpu.SMEM(lengths.shape, jnp.int32),
            pltpu.VMEM((rows, features), bf16),
            pltpu.VMEM((1, features), f32),
            pltpu.VMEM((1, rows), jnp.int32),
            pltpu.VMEM((8 * width, features), bf16),
            pltpu.VMEM((NZ * lanes, features), bf16),
            pltpu.VMEM((NZ * lanes, features), bf16),
            pltpu.VMEM((NZ, 8, lanes), jnp.int32),
            pltpu.VMEM((4, 8, 2 * lanes), jnp.int32),
            pltpu.VMEM((NY, 8, features), bf16),
            pltpu.VMEM((NZ, NY, features), bf16),
            pltpu.VMEM((8, features), f32),
            pltpu.VMEM((4, 4, 8, 2 * lanes), f32),
            pltpu.VMEM((NZ, 8, lanes), f32),
            pltpu.VMEM((NZ, 8, lanes), f32),
            pltpu.VMEM((8, lanes), f32),
            pltpu.VMEM((NX * NC, 8, lanes), f32),
            pltpu.SemaphoreType.DMA((len(NUMBER),)),
            pltpu.SemaphoreType.DMA((len(NUMBER),)),
            pltpu.SemaphoreType.DMA((8,)),
            pltpu.SemaphoreType.REGULAR((RELAYS,)),
        ],
        compiler_params=pltpu.CompilerParams(
            collective_id=0, has_side_effects=True, vmem_limit_bytes=64 * 2**20
        ),
    )(
        lengths, prior_device, prior_row, hidden, norm_gain.reshape(1, features), head_weight.T,
        targets.reshape(1, rows),
    )
    return logprob.reshape(rows), entropy.reshape(rows)


def solution(mesh):
    in_specs = (P("tok", None), P(), P(None, ("tok", "voc")), P("tok"), P(), P(), P())
    out_specs = (P("tok"), P("tok"))
    return jax.shard_map(body, mesh=mesh, in_specs=in_specs, out_specs=out_specs, check_vma=False)
```

```python
import jax
import jax.numpy as jnp
from jax import lax
from jax.experimental import pallas as pl
from jax.experimental.pallas import tpu as pltpu
from jax.sharding import PartitionSpec as P

epsilon = 1e-05
MESH = pl.DeviceIdType.MESH
NZ, NY, NX, NC = 8, 4, 4, 2
OFF = (0, -1, 1, -2, 2, -3, 3, 4)
MIRROR = (0, 2, 1, 4, 3, 6, 5, 7)
HALF, PIECE = 64, 32
KEPT = (None, 128, 192, 384, 448, 640, 704, 896)
SWAPPED = (None, 256, 320, 512, 576, 768, 832, 960)
LOWEST = -1e30


def message_numbers():
    names = ["own_s"] + [(side, part) for side in "rl" for part in ("a", "b", "f0", "f1", "f2")]
    names += [("share", d, q) for d in range(1, 3) for q in (0, 2)]
    names += [("share", 3, q, step) for q in (0, 2) for step in range(3)]
    names += [("z", side, k, p) for side in "rl" for k in range(4) for p in range(2)]
    names += [("x", s, p) for s in range(1, NZ) for p in range(2)]
    names += [("target", s) for s in range(1, NZ)]
    names += [("row_y", d) for d in range(1, NY)]
    names += [("row_z", s) for s in range(1, NZ)]
    names += [("stat_z", s) for s in range(1, NZ)]
    names += [("stat_v", i, j) for i in range(NX) for j in range(NC) if i + j]
    return {name: at for at, name in enumerate(names)}


NUMBER = message_numbers()


def peer(dx=0, dy=0, dz=0, dc=0):
    tok, voc = lax.axis_index("tok"), lax.axis_index("voc")
    z, y, x, c = tok // NY, tok % NY, voc // NC, voc % NC
    return (
        ((z + dz + NZ) % NZ) * NY + (y + dy + NY) % NY,
        ((x + dx + NX) % NX) * NC + (c + dc) % NC,
    )


PEERS = [dict(dx=1), dict(dx=-1), dict(dz=1), dict(dz=-1), dict(dc=1)] + [dict(dy=d) for d in range(1, NY)]
RELAYS = 4


def kernel(
    lengths_hbm, device_hbm, row_hbm, hidden_hbm, gain_hbm, weight, targets_hbm,
    logprob, entropy,
    lengths, prior_device, prior_row, hidden, gain, targets,
    wbuf, tbuf, gbuf, tgt, wanted, row_y, row_z, prior, stats, mine_z, got_z, mine_v, got_v,
    send, recv, local, relay,
):
    tok, voc = lax.axis_index("tok"), lax.axis_index("voc")
    z, y, x, c = tok // NY, tok % NY, voc // NC, voc % NC
    kind = x % 2
    width = weight.shape[0]
    half = width // 2
    third = half // 3
    wide = 2 * width
    block = 2 * HALF

    own_rows = pl.ds(pl.multiple_of(c * block, block), block)
    other_rows = pl.ds(pl.multiple_of((1 - c) * block, block), block)
    fetches = [
        pltpu.make_async_copy(weight, wbuf.at[pl.ds(0, width)], local.at[0]),
        pltpu.make_async_copy(hidden_hbm.at[own_rows], hidden.at[own_rows], local.at[1]),
        pltpu.make_async_copy(gain_hbm, gain.at[0], local.at[2]),
        pltpu.make_async_copy(hidden_hbm.at[other_rows], hidden.at[other_rows], local.at[3]),
        pltpu.make_async_copy(device_hbm, prior_device, local.at[4]),
        pltpu.make_async_copy(row_hbm, prior_row, local.at[5]),
        pltpu.make_async_copy(targets_hbm, targets, local.at[6]),
        pltpu.make_async_copy(lengths_hbm, lengths, local.at[7]),
    ]
    barrier = pltpu.get_barrier_semaphore()
    for offsets in PEERS:
        pl.semaphore_signal(barrier, inc=1, device_id=peer(**offsets), device_id_type=MESH)
    for fetch in fetches:
        fetch.start()

    def copy(name, source, target, **offsets):
        at = NUMBER[name]
        return pltpu.make_async_remote_copy(
            src_ref=source, dst_ref=target, send_sem=send.at[at], recv_sem=recv.at[at],
            device_id=peer(**offsets), device_id_type=MESH,
        )

    def part_row(d, q):
        return d * wide + q * half

    def weights(name):
        if name == "own_s":
            source, target, rows, offsets = 0, width, width, dict(dc=1)
        elif name[0] == "share" and name[1] == 3:
            step = name[3] * third
            source, target, rows = part_row(3, name[2]) + step, part_row(3, name[2] + 1) + step, third
            offsets = dict(dc=1)
        elif name[0] == "share":
            source, target, rows = part_row(name[1], name[2]), part_row(name[1], name[2] + 1), half
            offsets = dict(dc=1)
        else:
            side, part = name
            q, offsets = (0, dict(dy=1)) if side == "r" else (2, dict(dy=-1))
            first = 0 if side == "r" else half
            if part == "b":
                source, target, rows = half - first, part_row(2, q), half
            elif part == "a":
                source, target, rows = first, part_row(1, q), half
            else:
                step = int(part[1]) * third
                source, target, rows = part_row(1, q) + step, part_row(3, q) + step, third
        return copy(name, wbuf.at[pl.ds(source, rows)], wbuf.at[pl.ds(target, rows)], **offsets)

    source_slot = {"r": (0, 1, 3, 5), "l": (0, 2, 4, 6)}
    target_slot = {"r": (1, 3, 5, 7), "l": (2, 4, 6, 7)}

    def piece(start, p):
        return tbuf.at[pl.ds(start + p * PIECE, PIECE)]

    def along_z(side, k, p):
        if k:
            source = piece(KEPT[source_slot[side][k]], p)
        else:
            source = tbuf.at[pl.ds(pl.multiple_of(kind * HALF + p * PIECE, PIECE), PIECE)]
        return copy(
            ("z", side, k, p), source, piece(KEPT[target_slot[side][k]], p), dz=1 if side == "r" else -1
        )

    def along_x(s, p):
        return copy(("x", s, p), piece(KEPT[s], p), piece(SWAPPED[s], p), dx=1 if p == 0 else -1)

    def target_message(s):
        return copy(("target", s), tgt.at[0], tgt.at[MIRROR[s]], dz=OFF[s])

    def row_y_message(d):
        return copy(("row_y", d), row_y.at[0], row_y.at[d], dy=d)

    def row_z_message(s):
        return copy(("row_z", s), row_z.at[z], row_z.at[z], dz=OFF[s])

    def row_z_arrival(s):
        origin = (z - OFF[s] + NZ) % NZ
        return copy(("row_z", s), row_z.at[origin], row_z.at[origin], dz=OFF[s])

    def stat_z_message(s):
        return copy(("stat_z", s), mine_z.at[s], got_z.at[MIRROR[s]], dz=OFF[s])

    def stat_v_message(i, j):
        return copy(("stat_v", i, j), mine_v, got_v.at[voc], dx=i, dc=j)

    def stat_v_arrival(i, j):
        origin = ((x - i + NX) % NX) * NC + (c + j) % NC
        return copy(("stat_v", i, j), got_v.at[origin], got_v.at[origin], dx=i, dc=j)

    sent = []

    def start(make, *which):
        make(*which).start()
        sent.append((make, which))

    def norm(rows):
        mean = jnp.sum(rows * rows, axis=1, keepdims=True) / rows.shape[1]
        return rows * lax.rsqrt(mean + epsilon) * gain[...]

    def norm_half(which):
        low = pl.multiple_of(c * block + which * HALF, HALF)
        rows = norm(hidden[pl.ds(low, HALF), :].astype(jnp.float32))
        tbuf[pl.ds(pl.multiple_of(which * HALF, HALF), HALF), :] = rows.astype(jnp.bfloat16)

    for fetch in fetches[1:]:
        fetch.wait()
    norm_half(kind)
    asked = jnp.int32(0)
    for t in range(NZ * NY):
        asked = asked + jnp.where(prior_device[t] == tok, prior_row[t], 0)
    shape = (8, hidden.shape[0])
    chosen = (lax.broadcasted_iota(jnp.int32, shape, 0) == y) & (lax.broadcasted_iota(jnp.int32, shape, 1) == asked)
    outgoing = jnp.dot(
        jnp.where(chosen, 1.0, 0.0).astype(jnp.bfloat16), hidden[...], preferred_element_type=jnp.float32
    )
    row_y[0] = norm(outgoing).astype(jnp.bfloat16)
    fetches[0].wait()

    pl.semaphore_wait(barrier, len(PEERS))
    for d in range(1, NY):
        start(row_y_message, d)
    for p in range(2):
        start(along_z, "r", 0, p)
        start(along_z, "l", 0, 1 - p)
    for part in "ab":
        for side in "rl":
            start(weights, (side, part))
    start(weights, "own_s")

    def tell(level, axis):
        for d in (1, -1):
            pl.semaphore_signal(relay.at[level], inc=1, device_id=peer(**{axis: d}), device_id_type=MESH)

    tell(0, "dz")
    tell(3, "dx")

    def turned(value):
        return jnp.where(kind == 0, value, pltpu.roll(value, HALF, 1))

    shifted = pltpu.roll(jnp.broadcast_to(targets[...], shape), shape[1] - 1, 1)
    straight = jnp.where(c == 0, shifted[:, :block], shifted[:, block:])
    tgt[0] = turned(straight)
    def pass_on(k, late):
        for side in "rl":
            p = late if side == "r" else 1 - late
            along_z(side, k, p).wait_recv()
            if k < 2 or (k == 2 and late == 0):
                start(along_z, side, k + 1, p)
            start(along_x, target_slot[side][k], p)

    pl.semaphore_wait(relay.at[0], 2)
    tell(1, "dz")
    norm_half(1 - kind)
    pl.semaphore_wait(relay.at[1], 2)
    tell(2, "dz")
    for d in range(1, NY):
        row_y_message(d).wait_recv()
    gathered = row_y[0].astype(jnp.float32)
    for d in range(1, NY):
        gathered = gathered + row_y[d].astype(jnp.float32)
    pl.semaphore_wait(relay.at[3], 2)
    pl.semaphore_wait(relay.at[2], 2)

    @pl.when(c == 1)
    def _():
        row_z[z] = gathered[:NY].astype(jnp.bfloat16)
        for s in range(1, NZ):
            row_z_message(s).start()

    for s in range(1, NZ):
        start(target_message, s)
    prior[...] = jnp.zeros_like(prior)
    for g in range(4):
        stats[g, 0] = jnp.full(stats.shape[2:], LOWEST, jnp.float32)
        for k in range(1, 4):
            stats[g, k] = jnp.zeros(stats.shape[2:], jnp.float32)

    def whole(slot):
        for p in range(2):
            along_x(slot, p).wait_recv()

    def assemble(g):
        rows = 2 * block
        gbuf[g * rows : (g + 1) * rows] = tbuf[g * rows : (g + 1) * rows]
        tails = [(HALF, 0, 1)] if g == 0 else []
        tails += [(KEPT[s], s, kind) for s in range(1, NZ)] + [(SWAPPED[s], s, 1 - kind) for s in range(1, NZ)]
        for low, s, which in tails:
            if low // rows == g:
                last = tbuf[low + HALF - 16 : low + HALF].astype(jnp.float32)
                here = (lax.broadcasted_iota(jnp.int32, last.shape, 0) == 15) & (c * which == 1)
                last = jnp.where(here, jnp.broadcast_to(prior[s : s + 1, :], last.shape), last)
                gbuf[low + HALF - 16 : low + HALF] = last.astype(jnp.bfloat16)

    lane = lax.broadcasted_iota(jnp.int32, (8, block), 1)

    def kept_pair(first, second):
        return jnp.where(lane < HALF, first, pltpu.roll(second, HALF, 1))

    def swapped_pair(first, second):
        return jnp.where(lane < HALF, pltpu.roll(first, HALF, 1), second)

    def unit(g, d):
        rows = 2 * block
        w = wbuf[pl.ds(pl.multiple_of(d * wide, wide), wide), :]
        t = gbuf[pl.ds(pl.multiple_of(g * rows, rows), rows), :]
        logits = lax.dot_general(w, t, (((1,), (1,)), ((), ())), preferred_element_type=jnp.float32)
        logits = logits.reshape(wide // 8, 8, rows)
        old = stats[g, 0]
        top = jnp.maximum(old, jnp.max(logits, axis=0))
        scale = jnp.exp(old - top)
        e = jnp.exp(logits - top[None])
        stats[g, 0] = top
        stats[g, 1] = stats[g, 1] * scale + jnp.sum(e, axis=0)
        stats[g, 2] = stats[g, 2] * scale + jnp.sum(e * logits, axis=0)
        picked = stats[g, 3]
        each = half // 8
        for q in range(4):
            side = jnp.where(d == 0, 0, jnp.where(d == 3, 2, 3 if q < 2 else 1))
            core = jnp.where(d == 0, q // 2, q % 2)
            part = jnp.where(d == 0, q % 2, jnp.where(d == 2, 1 - q // 2, q // 2))
            device = (z * NY + (y + side) % NY) * (NX * NC) + x * NC + (c + core) % NC
            at = lax.broadcasted_iota(jnp.int32, (each, 8, rows), 0) * 8
            hit = at == (wanted[g] - (device * width + part * half))[None]
            picked = picked + jnp.sum(jnp.where(hit, logits[q * each : (q + 1) * each], 0.0), axis=0)
        stats[g, 3] = picked

    sub = lax.broadcasted_iota(jnp.int32, (8, block), 0)

    def tile(top, total, moment, picked):
        return jnp.where(sub == 0, top, jnp.where(sub == 1, total, jnp.where(sub == 2, moment, picked)))

    def reduced(g, which):
        lanes = slice(which * block, (which + 1) * block)
        tops = stats[g, 0, :, lanes]
        top = jnp.max(tops, axis=0, keepdims=True)
        scale = jnp.exp(tops - top)
        return tile(
            top,
            jnp.sum(stats[g, 1, :, lanes] * scale, axis=0, keepdims=True),
            jnp.sum(stats[g, 2, :, lanes] * scale, axis=0, keepdims=True),
            jnp.sum(stats[g, 3, :, lanes], axis=0, keepdims=True),
        )

    def give_pair(g):
        kept, swapped = reduced(g, 1), reduced(g + 1, 0)
        mine_z[2 * g + 1] = kept_pair(kept, swapped)
        mine_z[2 * g + 2] = jnp.where(lane < HALF, pltpu.roll(kept, HALF, 1), swapped)

    def units(k, carry):
        @pl.when(k == 0)
        def _():
            pass_on(0, 0)
            pass_on(0, 1)
            for q, side in ((0, "r"), (2, "l")):
                weights((side, "a")).wait_recv()
                for step in range(3):
                    start(weights, (side, f"f{step}"))
                start(weights, ("share", 1, q))
            pass_on(1, 0)
            pass_on(1, 1)
            weights("own_s").wait_recv()
            for s in range(1, NZ):
                target_message(s).wait_recv()
            pairs = [(s, s + 1) for s in (1, 3, 5)]
            kept = [kept_pair(tgt[i], tgt[j]) for i, j in pairs]
            swapped = [swapped_pair(tgt[i], tgt[j]) for i, j in pairs]
            for g, both in enumerate(zip([straight] + swapped, kept + [tgt[7]])):
                place = lax.broadcasted_iota(jnp.int32, (8, 2 * block), 0)
                wanted[g] = jnp.concatenate(both, axis=1) - place

            @pl.when(c == 1)
            def _():
                for s in range(1, NZ):
                    row_z_arrival(s).wait_recv()
                shape = (8, NZ * NY)
                wants = jnp.full(shape, -1, jnp.int32)
                place = lax.broadcasted_iota(jnp.int32, shape, 0)
                for s in range(NZ):
                    turn = ((z + OFF[s] + NZ) % NZ) * NY + y
                    wants = jnp.where(place == s, prior_device[turn], wants)
                across = lax.broadcasted_iota(jnp.int32, shape, 1)
                pick = jnp.where(wants == across, 1.0, 0.0).astype(jnp.bfloat16)
                table = row_z[...].reshape(NZ * NY, row_z.shape[2])
                prior[...] = jnp.dot(pick, table, preferred_element_type=jnp.float32)

            whole(1)
            whole(2)
            assemble(0)
            assemble(1)

        @pl.when(k == 2)
        def _():
            pass_on(2, 0)
            weights(("share", 1, 0)).wait_recv()
            weights(("share", 1, 2)).wait_recv()

        @pl.when(k == 4)
        def _():
            pass_on(2, 1)
            for q, side in ((0, "r"), (2, "l")):
                weights((side, "b")).wait_recv()
                start(weights, ("share", 2, q))
            whole(3)
            whole(4)
            assemble(2)

        def share_far(step):
            for q, side in ((0, "r"), (2, "l")):
                weights((side, f"f{step}")).wait_recv()
                start(weights, ("share", 3, q, step))

        @pl.when(k == 6)
        def _():
            along_z("r", 3, 0).wait_recv()
            start(along_x, 7, 0)
            along_z("l", 3, 1).wait_recv()
            start(along_x, 7, 1)
            share_far(0)
            for q in (0, 2):
                weights(("share", 2, q)).wait_recv()

        @pl.when(k == 8)
        def _():
            share_far(1)

        @pl.when(k == 9)
        def _():
            whole(5)
            whole(6)
            whole(7)
            assemble(3)

        @pl.when(k == 10)
        def _():
            share_far(2)

        @pl.when(k == 12)
        def _():
            for q in (0, 2):
                for step in range(3):
                    weights(("share", 3, q, step)).wait_recv()

        @pl.when(k == 13)
        def _():
            mine_z[7] = reduced(3, 1)
            start(stat_z_message, 7)

        @pl.when(k == 14)
        def _():
            give_pair(2)
            start(stat_z_message, 5)
            start(stat_z_message, 6)

        @pl.when(k == 15)
        def _():
            give_pair(1)
            start(stat_z_message, 3)
            start(stat_z_message, 4)

        early = jnp.where(k < 4, k % 2, jnp.where(k < 6, 2, k - 6))
        unit(
            jnp.where(k < 9, early, jnp.where(k < 12, 3, 15 - k)),
            jnp.where(k < 4, k // 2, jnp.where(k < 6, k - 4, jnp.where(k < 9, 2, jnp.where(k < 12, k - 9, 3)))),
        )
        return carry

    lax.fori_loop(0, 16, units, 0)
    give_pair(0)
    start(stat_z_message, 1)
    start(stat_z_message, 2)
    mine_z[0] = turned(reduced(0, 0))

    def merge(tiles):
        top = tiles[0][0:1]
        for other in tiles[1:]:
            top = jnp.maximum(top, other[0:1])
        total, moment, picked = 0.0, 0.0, 0.0
        for one in tiles:
            scale = jnp.exp(one[0:1] - top)
            total = total + one[1:2] * scale
            moment = moment + one[2:3] * scale
            picked = picked + one[3:4]
        return top, total, moment, picked

    for s in range(1, NZ):
        stat_z_message(s).wait_recv()
    merged = turned(tile(*merge([mine_z[0]] + [got_z[s] for s in range(1, NZ)])))
    mine_v[...] = merged
    for i in range(NX):
        for j in range(NC):
            if i + j:
                start(stat_v_message, i, j)
    got_v[voc] = merged
    for i in range(NX):
        for j in range(NC):
            if i + j:
                stat_v_arrival(i, j).wait_recv()
    row_of, entropy_of = [], []
    for h in range(NC):
        top, total, moment, picked = merge([got_v[i * NC + h] for i in range(NX)])
        normalizer = top + jnp.log(total)
        row_of.append(picked - normalizer)
        entropy_of.append(normalizer - moment / total)
    live = lax.broadcasted_iota(jnp.int32, (1, 2 * block), 1) < lengths[tok]

    def finished(parts):
        both = jnp.broadcast_to(jnp.concatenate(parts, axis=1), (8, 2 * block))
        return jnp.where(live, pltpu.roll(both, 1, 1)[0:1], 0.0)

    logprob[...] = finished(row_of)
    entropy[...] = finished(entropy_of)

    for make, which in sent:
        make(*which).wait_send()

    @pl.when(c == 1)
    def _():
        for s in range(1, NZ):
            row_z_message(s).wait_send()


def body(hidden, norm_gain, head_weight, targets, lengths, prior_device, prior_row):
    rows, features = hidden.shape
    width = head_weight.shape[1]
    vmem, hbm = pl.BlockSpec(memory_space=pltpu.VMEM), pl.BlockSpec(memory_space=pltpu.HBM)
    f32, bf16 = jnp.float32, jnp.bfloat16
    out = jax.ShapeDtypeStruct((1, rows), f32)
    lanes = 2 * HALF
    logprob, entropy = pl.pallas_call(
        kernel,
        out_shape=(out, out),
        in_specs=[hbm] * 7,
        out_specs=(vmem, vmem),
        scratch_shapes=[
            pltpu.SMEM(lengths.shape, jnp.int32),
            pltpu.SMEM(lengths.shape, jnp.int32),
            pltpu.SMEM(lengths.shape, jnp.int32),
            pltpu.VMEM((rows, features), bf16),
            pltpu.VMEM((1, features), f32),
            pltpu.VMEM((1, rows), jnp.int32),
            pltpu.VMEM((8 * width, features), bf16),
            pltpu.VMEM((NZ * lanes, features), bf16),
            pltpu.VMEM((NZ * lanes, features), bf16),
            pltpu.VMEM((NZ, 8, lanes), jnp.int32),
            pltpu.VMEM((4, 8, 2 * lanes), jnp.int32),
            pltpu.VMEM((NY, 8, features), bf16),
            pltpu.VMEM((NZ, NY, features), bf16),
            pltpu.VMEM((8, features), f32),
            pltpu.VMEM((4, 4, 8, 2 * lanes), f32),
            pltpu.VMEM((NZ, 8, lanes), f32),
            pltpu.VMEM((NZ, 8, lanes), f32),
            pltpu.VMEM((8, lanes), f32),
            pltpu.VMEM((NX * NC, 8, lanes), f32),
            pltpu.SemaphoreType.DMA((len(NUMBER),)),
            pltpu.SemaphoreType.DMA((len(NUMBER),)),
            pltpu.SemaphoreType.DMA((8,)),
            pltpu.SemaphoreType.REGULAR((RELAYS,)),
        ],
        compiler_params=pltpu.CompilerParams(
            collective_id=0, has_side_effects=True, vmem_limit_bytes=48 * 2**20
        ),
    )(
        *[
            pltpu.with_memory_space_constraint(operand, pltpu.HBM)
            for operand in (
                lengths, prior_device, prior_row, hidden, norm_gain, head_weight.T, targets.reshape(1, rows)
            )
        ]
    )
    return logprob.reshape(rows), entropy.reshape(rows)


def solution(mesh):
    in_specs = (P("tok", None), P(), P(None, ("tok", "voc")), P("tok"), P(), P(), P())
    out_specs = (P("tok"), P("tok"))
    return jax.shard_map(body, mesh=mesh, in_specs=in_specs, out_specs=out_specs, check_vma=False)
```

```python
import jax
import jax.numpy as jnp
from jax import lax
from jax.experimental import pallas as pl
from jax.experimental.pallas import tpu as pltpu
from jax.sharding import PartitionSpec as P

epsilon = 1e-05
MESH = pl.DeviceIdType.MESH
NZ, NY, NX, NC = 8, 4, 4, 2
OFF = (0, -1, 1, -2, 2, -3, 3, 4)
MIRROR = (0, 2, 1, 4, 3, 6, 5, 7)
HALF, PIECE = 64, 32
KEPT = (None, 128, 192, 384, 448, 640, 704, 896)
SWAPPED = (None, 256, 320, 512, 576, 768, 832, 960)
LOWEST = -1e30


def message_numbers():
    names = ["own_s"] + [(side, part) for side in "rl" for part in ("a", "b", "f0", "f1", "f2")]
    names += [("share", d, q) for d in range(1, 3) for q in (0, 2)]
    names += [("share", 3, q, step) for q in (0, 2) for step in range(3)]
    names += [("z", side, k, p) for side in "rl" for k in range(4) for p in range(2)]
    names += [("x", s, p) for s in range(1, NZ) for p in range(2)]
    names += [("target", s) for s in range(1, NZ)]
    names += [("row_y", d) for d in range(1, NY)]
    names += [("row_z", s) for s in range(1, NZ)]
    names += [("stat_z", s) for s in range(1, NZ)]
    names += [("stat_v", i, j) for i in range(NX) for j in range(NC) if i + j]
    return {name: at for at, name in enumerate(names)}


NUMBER = message_numbers()


def peer(dx=0, dy=0, dz=0, dc=0):
    tok, voc = lax.axis_index("tok"), lax.axis_index("voc")
    z, y, x, c = tok // NY, tok % NY, voc // NC, voc % NC
    return (
        ((z + dz + NZ) % NZ) * NY + (y + dy + NY) % NY,
        ((x + dx + NX) % NX) * NC + (c + dc) % NC,
    )


PEERS = [dict(dx=1), dict(dx=-1), dict(dz=1), dict(dz=-1), dict(dc=1)] + [dict(dy=d) for d in range(1, NY)]
RELAYS = 4


def kernel(
    lengths_hbm, device_hbm, row_hbm, hidden_hbm, gain_hbm, weight, targets_hbm,
    logprob, entropy,
    lengths, prior_device, prior_row, hidden, gain, targets,
    wbuf, tbuf, gbuf, tgt, wanted, row_y, row_z, prior, stats, mine_z, got_z, mine_v, got_v,
    send, recv, local, relay,
):
    tok, voc = lax.axis_index("tok"), lax.axis_index("voc")
    z, y, x, c = tok // NY, tok % NY, voc // NC, voc % NC
    kind = x % 2
    width = weight.shape[0]
    half = width // 2
    third = half // 3
    wide = 2 * width
    block = 2 * HALF

    own_rows = pl.ds(pl.multiple_of(c * block, block), block)
    other_rows = pl.ds(pl.multiple_of((1 - c) * block, block), block)
    fetches = [
        pltpu.make_async_copy(weight, wbuf.at[pl.ds(0, width)], local.at[0]),
        pltpu.make_async_copy(hidden_hbm.at[own_rows], hidden.at[own_rows], local.at[1]),
        pltpu.make_async_copy(gain_hbm, gain.at[0], local.at[2]),
        pltpu.make_async_copy(hidden_hbm.at[other_rows], hidden.at[other_rows], local.at[3]),
        pltpu.make_async_copy(device_hbm, prior_device, local.at[4]),
        pltpu.make_async_copy(row_hbm, prior_row, local.at[5]),
        pltpu.make_async_copy(targets_hbm, targets, local.at[6]),
        pltpu.make_async_copy(lengths_hbm, lengths, local.at[7]),
    ]
    barrier = pltpu.get_barrier_semaphore()
    for offsets in PEERS:
        pl.semaphore_signal(barrier, inc=1, device_id=peer(**offsets), device_id_type=MESH)
    for fetch in fetches:
        fetch.start()

    def copy(name, source, target, **offsets):
        at = NUMBER[name]
        return pltpu.make_async_remote_copy(
            src_ref=source, dst_ref=target, send_sem=send.at[at], recv_sem=recv.at[at],
            device_id=peer(**offsets), device_id_type=MESH,
        )

    def part_row(d, q):
        return d * wide + q * half

    def weights(name):
        if name == "own_s":
            source, target, rows, offsets = 0, width, width, dict(dc=1)
        elif name[0] == "share" and name[1] == 3:
            step = name[3] * third
            source, target, rows = part_row(3, name[2]) + step, part_row(3, name[2] + 1) + step, third
            offsets = dict(dc=1)
        elif name[0] == "share":
            source, target, rows = part_row(name[1], name[2]), part_row(name[1], name[2] + 1), half
            offsets = dict(dc=1)
        else:
            side, part = name
            q, offsets = (0, dict(dy=1)) if side == "r" else (2, dict(dy=-1))
            first = 0 if side == "r" else half
            if part == "b":
                source, target, rows = half - first, part_row(2, q), half
            elif part == "a":
                source, target, rows = first, part_row(1, q), half
            else:
                step = int(part[1]) * third
                source, target, rows = part_row(1, q) + step, part_row(3, q) + step, third
        return copy(name, wbuf.at[pl.ds(source, rows)], wbuf.at[pl.ds(target, rows)], **offsets)

    source_slot = {"r": (0, 1, 3, 5), "l": (0, 2, 4, 6)}
    target_slot = {"r": (1, 3, 5, 7), "l": (2, 4, 6, 7)}

    def piece(start, p):
        return tbuf.at[pl.ds(start + p * PIECE, PIECE)]

    def along_z(side, k, p):
        if k:
            source = piece(KEPT[source_slot[side][k]], p)
        else:
            source = tbuf.at[pl.ds(pl.multiple_of(kind * HALF + p * PIECE, PIECE), PIECE)]
        return copy(
            ("z", side, k, p), source, piece(KEPT[target_slot[side][k]], p), dz=1 if side == "r" else -1
        )

    def along_x(s, p):
        return copy(("x", s, p), piece(KEPT[s], p), piece(SWAPPED[s], p), dx=1 if p == 0 else -1)

    def target_message(s):
        return copy(("target", s), tgt.at[0], tgt.at[MIRROR[s]], dz=OFF[s])

    def row_y_message(d):
        return copy(("row_y", d), row_y.at[0], row_y.at[d], dy=d)

    def row_z_message(s):
        return copy(("row_z", s), row_z.at[z], row_z.at[z], dz=OFF[s])

    def row_z_arrival(s):
        origin = (z - OFF[s] + NZ) % NZ
        return copy(("row_z", s), row_z.at[origin], row_z.at[origin], dz=OFF[s])

    def stat_z_message(s):
        return copy(("stat_z", s), mine_z.at[s], got_z.at[MIRROR[s]], dz=OFF[s])

    def stat_v_message(i, j):
        return copy(("stat_v", i, j), mine_v, got_v.at[voc], dx=i, dc=j)

    def stat_v_arrival(i, j):
        origin = ((x - i + NX) % NX) * NC + (c + j) % NC
        return copy(("stat_v", i, j), got_v.at[origin], got_v.at[origin], dx=i, dc=j)

    sent = []

    def start(make, *which):
        make(*which).start()
        sent.append((make, which))

    def norm(rows):
        mean = jnp.sum(rows * rows, axis=1, keepdims=True) / rows.shape[1]
        return rows * lax.rsqrt(mean + epsilon) * gain[...]

    def norm_half(which):
        low = pl.multiple_of(c * block + which * HALF, HALF)
        rows = norm(hidden[pl.ds(low, HALF), :].astype(jnp.float32))
        tbuf[pl.ds(pl.multiple_of(which * HALF, HALF), HALF), :] = rows.astype(jnp.bfloat16)

    for fetch in fetches[1:]:
        fetch.wait()
    norm_half(kind)
    asked = jnp.int32(0)
    for t in range(NZ * NY):
        asked = asked + jnp.where(prior_device[t] == tok, prior_row[t], 0)
    shape = (8, hidden.shape[0])
    chosen = (lax.broadcasted_iota(jnp.int32, shape, 0) == y) & (lax.broadcasted_iota(jnp.int32, shape, 1) == asked)
    outgoing = jnp.dot(
        jnp.where(chosen, 1.0, 0.0).astype(jnp.bfloat16), hidden[...], preferred_element_type=jnp.float32
    )
    row_y[0] = norm(outgoing).astype(jnp.bfloat16)
    fetches[0].wait()

    pl.semaphore_wait(barrier, len(PEERS))
    def tell(level, axis):
        for d in (1, -1):
            pl.semaphore_signal(relay.at[level], inc=1, device_id=peer(**{axis: d}), device_id_type=MESH)

    tell(0, "dz")
    tell(3, "dx")

    for d in range(1, NY):
        start(row_y_message, d)
    for p in range(2):
        start(along_z, "r", 0, p)
        start(along_z, "l", 0, 1 - p)
    for part in "ab":
        for side in "rl":
            start(weights, (side, part))
    start(weights, "own_s")

    def turned(value):
        return jnp.where(kind == 0, value, pltpu.roll(value, HALF, 1))

    shifted = pltpu.roll(jnp.broadcast_to(targets[...], shape), shape[1] - 1, 1)
    straight = jnp.where(c == 0, shifted[:, :block], shifted[:, block:])
    tgt[0] = turned(straight)
    def pass_on(k, late):
        for side in "rl":
            p = late if side == "r" else 1 - late
            along_z(side, k, p).wait_recv()
            if k < 2 or (k == 2 and late == 0):
                start(along_z, side, k + 1, p)
            start(along_x, target_slot[side][k], p)

    pl.semaphore_wait(relay.at[0], 2)
    tell(1, "dz")
    pl.semaphore_wait(relay.at[1], 2)
    tell(2, "dz")
    norm_half(1 - kind)
    for d in range(1, NY):
        row_y_message(d).wait_recv()
    gathered = row_y[0].astype(jnp.float32)
    for d in range(1, NY):
        gathered = gathered + row_y[d].astype(jnp.float32)
    pl.semaphore_wait(relay.at[3], 2)
    pl.semaphore_wait(relay.at[2], 2)

    @pl.when(c == 1)
    def _():
        row_z[z] = gathered[:NY].astype(jnp.bfloat16)
        for s in range(1, NZ):
            row_z_message(s).start()

    for s in range(1, NZ):
        start(target_message, s)
    prior[...] = jnp.zeros_like(prior)
    for g in range(4):
        stats[g, 0] = jnp.full(stats.shape[2:], LOWEST, jnp.float32)
        for k in range(1, 4):
            stats[g, k] = jnp.zeros(stats.shape[2:], jnp.float32)

    def whole(slot):
        for p in range(2):
            along_x(slot, p).wait_recv()

    def assemble(g):
        rows = 2 * block
        gbuf[g * rows : (g + 1) * rows] = tbuf[g * rows : (g + 1) * rows]
        tails = [(HALF, 0, 1)] if g == 0 else []
        tails += [(KEPT[s], s, kind) for s in range(1, NZ)] + [(SWAPPED[s], s, 1 - kind) for s in range(1, NZ)]
        for low, s, which in tails:
            if low // rows == g:
                last = tbuf[low + HALF - 16 : low + HALF].astype(jnp.float32)
                here = (lax.broadcasted_iota(jnp.int32, last.shape, 0) == 15) & (c * which == 1)
                last = jnp.where(here, jnp.broadcast_to(prior[s : s + 1, :], last.shape), last)
                gbuf[low + HALF - 16 : low + HALF] = last.astype(jnp.bfloat16)

    lane = lax.broadcasted_iota(jnp.int32, (8, block), 1)

    def kept_pair(first, second):
        return jnp.where(lane < HALF, first, pltpu.roll(second, HALF, 1))

    def swapped_pair(first, second):
        return jnp.where(lane < HALF, pltpu.roll(first, HALF, 1), second)

    def unit(g, d):
        rows = 2 * block
        w = wbuf[pl.ds(pl.multiple_of(d * wide, wide), wide), :]
        t = gbuf[pl.ds(pl.multiple_of(g * rows, rows), rows), :]
        logits = lax.dot_general(w, t, (((1,), (1,)), ((), ())), preferred_element_type=jnp.float32)
        logits = logits.reshape(wide // 8, 8, rows)
        old = stats[g, 0]
        top = jnp.maximum(old, jnp.max(logits, axis=0))
        scale = jnp.exp(old - top)
        e = jnp.exp(logits - top[None])
        stats[g, 0] = top
        stats[g, 1] = stats[g, 1] * scale + jnp.sum(e, axis=0)
        stats[g, 2] = stats[g, 2] * scale + jnp.sum(e * logits, axis=0)
        picked = stats[g, 3]
        each = half // 8
        for q in range(4):
            side = jnp.where(d == 0, 0, jnp.where(d == 3, 2, 3 if q < 2 else 1))
            core = jnp.where(d == 0, q // 2, q % 2)
            part = jnp.where(d == 0, q % 2, jnp.where(d == 2, 1 - q // 2, q // 2))
            device = (z * NY + (y + side) % NY) * (NX * NC) + x * NC + (c + core) % NC
            at = lax.broadcasted_iota(jnp.int32, (each, 8, rows), 0) * 8
            hit = at == (wanted[g] - (device * width + part * half))[None]
            picked = picked + jnp.sum(jnp.where(hit, logits[q * each : (q + 1) * each], 0.0), axis=0)
        stats[g, 3] = picked

    sub = lax.broadcasted_iota(jnp.int32, (8, block), 0)

    def tile(top, total, moment, picked):
        return jnp.where(sub == 0, top, jnp.where(sub == 1, total, jnp.where(sub == 2, moment, picked)))

    def reduced(g, which):
        lanes = slice(which * block, (which + 1) * block)
        tops = stats[g, 0, :, lanes]
        top = jnp.max(tops, axis=0, keepdims=True)
        scale = jnp.exp(tops - top)
        return tile(
            top,
            jnp.sum(stats[g, 1, :, lanes] * scale, axis=0, keepdims=True),
            jnp.sum(stats[g, 2, :, lanes] * scale, axis=0, keepdims=True),
            jnp.sum(stats[g, 3, :, lanes], axis=0, keepdims=True),
        )

    def give_pair(g):
        kept, swapped = reduced(g, 1), reduced(g + 1, 0)
        mine_z[2 * g + 1] = kept_pair(kept, swapped)
        mine_z[2 * g + 2] = jnp.where(lane < HALF, pltpu.roll(kept, HALF, 1), swapped)

    def units(k, carry):
        @pl.when(k == 0)
        def _():
            pass_on(0, 0)
            pass_on(0, 1)
            for q, side in ((0, "r"), (2, "l")):
                weights((side, "a")).wait_recv()
                for step in range(3):
                    start(weights, (side, f"f{step}"))
                start(weights, ("share", 1, q))
            pass_on(1, 0)
            pass_on(1, 1)
            weights("own_s").wait_recv()
            for s in range(1, NZ):
                target_message(s).wait_recv()
            pairs = [(s, s + 1) for s in (1, 3, 5)]
            kept = [kept_pair(tgt[i], tgt[j]) for i, j in pairs]
            swapped = [swapped_pair(tgt[i], tgt[j]) for i, j in pairs]
            for g, both in enumerate(zip([straight] + swapped, kept + [tgt[7]])):
                place = lax.broadcasted_iota(jnp.int32, (8, 2 * block), 0)
                wanted[g] = jnp.concatenate(both, axis=1) - place

            @pl.when(c == 1)
            def _():
                for s in range(1, NZ):
                    row_z_arrival(s).wait_recv()
                shape = (8, NZ * NY)
                wants = jnp.full(shape, -1, jnp.int32)
                place = lax.broadcasted_iota(jnp.int32, shape, 0)
                for s in range(NZ):
                    turn = ((z + OFF[s] + NZ) % NZ) * NY + y
                    wants = jnp.where(place == s, prior_device[turn], wants)
                across = lax.broadcasted_iota(jnp.int32, shape, 1)
                pick = jnp.where(wants == across, 1.0, 0.0).astype(jnp.bfloat16)
                table = row_z[...].reshape(NZ * NY, row_z.shape[2])
                prior[...] = jnp.dot(pick, table, preferred_element_type=jnp.float32)

            whole(1)
            whole(2)
            assemble(0)
            assemble(1)

        @pl.when(k == 2)
        def _():
            pass_on(2, 0)
            weights(("share", 1, 0)).wait_recv()
            weights(("share", 1, 2)).wait_recv()

        @pl.when(k == 4)
        def _():
            pass_on(2, 1)
            for q, side in ((0, "r"), (2, "l")):
                weights((side, "b")).wait_recv()
                start(weights, ("share", 2, q))
            whole(3)
            whole(4)
            assemble(2)

        def share_far(step):
            for q, side in ((0, "r"), (2, "l")):
                weights((side, f"f{step}")).wait_recv()
                start(weights, ("share", 3, q, step))

        @pl.when(k == 6)
        def _():
            along_z("r", 3, 0).wait_recv()
            start(along_x, 7, 0)
            along_z("l", 3, 1).wait_recv()
            start(along_x, 7, 1)
            share_far(0)
            for q in (0, 2):
                weights(("share", 2, q)).wait_recv()

        @pl.when(k == 8)
        def _():
            share_far(1)

        @pl.when(k == 9)
        def _():
            whole(5)
            whole(6)
            whole(7)
            assemble(3)

        @pl.when(k == 10)
        def _():
            share_far(2)

        @pl.when(k == 12)
        def _():
            for q in (0, 2):
                for step in range(3):
                    weights(("share", 3, q, step)).wait_recv()

        @pl.when(k == 13)
        def _():
            mine_z[7] = reduced(3, 1)
            start(stat_z_message, 7)

        @pl.when(k == 14)
        def _():
            give_pair(2)
            start(stat_z_message, 5)
            start(stat_z_message, 6)

        @pl.when(k == 15)
        def _():
            give_pair(1)
            start(stat_z_message, 3)
            start(stat_z_message, 4)

        early = jnp.where(k < 4, k % 2, jnp.where(k < 6, 2, k - 6))
        unit(
            jnp.where(k < 9, early, jnp.where(k < 12, 3, 15 - k)),
            jnp.where(k < 4, k // 2, jnp.where(k < 6, k - 4, jnp.where(k < 9, 2, jnp.where(k < 12, k - 9, 3)))),
        )
        return carry

    lax.fori_loop(0, 16, units, 0)
    give_pair(0)
    start(stat_z_message, 1)
    start(stat_z_message, 2)
    mine_z[0] = turned(reduced(0, 0))

    def merge(tiles):
        top = tiles[0][0:1]
        for other in tiles[1:]:
            top = jnp.maximum(top, other[0:1])
        total, moment, picked = 0.0, 0.0, 0.0
        for one in tiles:
            scale = jnp.exp(one[0:1] - top)
            total = total + one[1:2] * scale
            moment = moment + one[2:3] * scale
            picked = picked + one[3:4]
        return top, total, moment, picked

    for s in range(1, NZ):
        stat_z_message(s).wait_recv()
    merged = turned(tile(*merge([mine_z[0]] + [got_z[s] for s in range(1, NZ)])))
    mine_v[...] = merged
    for i in range(NX):
        for j in range(NC):
            if i + j:
                start(stat_v_message, i, j)
    got_v[voc] = merged
    for i in range(NX):
        for j in range(NC):
            if i + j:
                stat_v_arrival(i, j).wait_recv()
    row_of, entropy_of = [], []
    for h in range(NC):
        top, total, moment, picked = merge([got_v[i * NC + h] for i in range(NX)])
        normalizer = top + jnp.log(total)
        row_of.append(picked - normalizer)
        entropy_of.append(normalizer - moment / total)
    live = lax.broadcasted_iota(jnp.int32, (1, 2 * block), 1) < lengths[tok]

    def finished(parts):
        both = jnp.broadcast_to(jnp.concatenate(parts, axis=1), (8, 2 * block))
        return jnp.where(live, pltpu.roll(both, 1, 1)[0:1], 0.0)

    logprob[...] = finished(row_of)
    entropy[...] = finished(entropy_of)

    for make, which in sent:
        make(*which).wait_send()

    @pl.when(c == 1)
    def _():
        for s in range(1, NZ):
            row_z_message(s).wait_send()


def body(hidden, norm_gain, head_weight, targets, lengths, prior_device, prior_row):
    rows, features = hidden.shape
    width = head_weight.shape[1]
    vmem, hbm = pl.BlockSpec(memory_space=pltpu.VMEM), pl.BlockSpec(memory_space=pltpu.HBM)
    f32, bf16 = jnp.float32, jnp.bfloat16
    out = jax.ShapeDtypeStruct((1, rows), f32)
    lanes = 2 * HALF
    logprob, entropy = pl.pallas_call(
        kernel,
        out_shape=(out, out),
        in_specs=[hbm] * 7,
        out_specs=(vmem, vmem),
        scratch_shapes=[
            pltpu.SMEM(lengths.shape, jnp.int32),
            pltpu.SMEM(lengths.shape, jnp.int32),
            pltpu.SMEM(lengths.shape, jnp.int32),
            pltpu.VMEM((rows, features), bf16),
            pltpu.VMEM((1, features), f32),
            pltpu.VMEM((1, rows), jnp.int32),
            pltpu.VMEM((8 * width, features), bf16),
            pltpu.VMEM((NZ * lanes, features), bf16),
            pltpu.VMEM((NZ * lanes, features), bf16),
            pltpu.VMEM((NZ, 8, lanes), jnp.int32),
            pltpu.VMEM((4, 8, 2 * lanes), jnp.int32),
            pltpu.VMEM((NY, 8, features), bf16),
            pltpu.VMEM((NZ, NY, features), bf16),
            pltpu.VMEM((8, features), f32),
            pltpu.VMEM((4, 4, 8, 2 * lanes), f32),
            pltpu.VMEM((NZ, 8, lanes), f32),
            pltpu.VMEM((NZ, 8, lanes), f32),
            pltpu.VMEM((8, lanes), f32),
            pltpu.VMEM((NX * NC, 8, lanes), f32),
            pltpu.SemaphoreType.DMA((len(NUMBER),)),
            pltpu.SemaphoreType.DMA((len(NUMBER),)),
            pltpu.SemaphoreType.DMA((8,)),
            pltpu.SemaphoreType.REGULAR((RELAYS,)),
        ],
        compiler_params=pltpu.CompilerParams(
            collective_id=0, has_side_effects=True, vmem_limit_bytes=48 * 2**20
        ),
    )(
        *[
            pltpu.with_memory_space_constraint(operand, pltpu.HBM)
            for operand in (
                lengths, prior_device, prior_row, hidden, norm_gain, head_weight.T, targets.reshape(1, rows)
            )
        ]
    )
    return logprob.reshape(rows), entropy.reshape(rows)


def solution(mesh):
    in_specs = (P("tok", None), P(), P(None, ("tok", "voc")), P("tok"), P(), P(), P())
    out_specs = (P("tok"), P("tok"))
    return jax.shard_map(body, mesh=mesh, in_specs=in_specs, out_specs=out_specs, check_vma=False)
```
